32 devices in a mesh: job: 2 (over y), blk: 4 (over z), cell: 2 (over x), col: 2 (over core).
Axes of the slice: x: 2, y: 2, z: 4, core: 2. Of those that a mesh axis runs over, the one named last changes fastest.
Arguments:
- p_blocks: bfloat16 [64, 4, 2, 128, 128], P(('job', 'blk', 'cell')), parts along dimension 0, may hold values from -0.1875 to 0.1875
- p_cols: int32 [64, 4, 2], P(('job', 'blk', 'cell')), parts along dimension 0, may hold values from 0 to 7
- l_blocks: bfloat16 [64, 4, 2, 128, 128], P(('job', 'blk', 'cell')), parts along dimension 0, may hold values from -0.1875 to 0.1875
- l_cols: int32 [64, 4, 2], P(('job', 'blk', 'cell')), parts along dimension 0, may hold values from 0 to 7
- charges: bfloat16 [24, 2, 8192], P('col', None, ('job', 'blk', 'cell')), parts along dimension 2, may hold values from -6 to 6
- currents: bfloat16 [24, 2, 8192], P('col', None, ('job', 'blk', 'cell')), parts along dimension 2, may hold values from -6 to 6
- omegas: float32 [24], P('col'), may hold values from 0.5 to 4
- resist: float32 [8192], P(('job', 'blk', 'cell')), parts along dimension 0, may hold values from 0.05 to 2
- branch_ends: int32 [2, 8192], P(None, ('job', 'blk', 'cell')), parts along dimension 1, may hold values from 0 to 1023
Outputs:
- cell_rows: float32 [24, 2, 8192], P('col', None, ('job', 'blk', 'cell')), parts along dimension 2
- panel_rows: float32 [24, 2, 8192], P('col', None, ('job', 'blk', 'cell')), parts along dimension 2
The draws below stay inside these ranges and needn't reach their ends.
There are 2 independent parts, one for each index of `job`. The reference program is written for one: setup_inputs(seed, part) draws one part's arguments, and reference() takes and returns one part's arrays. A program takes and returns all parts, laid end to end along the dimension named above; an argument that names none is the same for every part. Nothing has to cross between parts.
Inputs may be any that keep to these rules, and one draw needn't show every extreme that they name: `p_cols`: block columns are numbered within the region of 8 blocks that the slot's region index names; repeats may occur. `l_cols`: as for p_cols. `branch_ends`: panel numbers within the cell's own region of 1024 panels; a cell may leave and enter the same panel.
All inputs are finite; a program needn't handle non-finite values.
Results may differ from the reference program's by a relative error of at most 0.0059.
Values may be sent and summed in bfloat16 or wider, within the bound.
A program may use at most 64 MiB of HBM per device.

```python
import math
import jax
import jax.numpy as jnp
from jax import lax

FREQS = 24
BS = 128
KP = 2
KL = 2
REG_BLOCKS = 8
REGION = 1024
NBLOCKS = 32
PANELS = 4096
CELLS = 4096
N_BLK = 4


def place_ends(values, own_key, smallest, largest):
    place = [jax.random.randint(jax.random.fold_in(own_key, axis), (), 0, length) for axis, length in enumerate(values.shape)]
    widest = values.shape.index(max(values.shape))
    beside = place[:widest] + [(place[widest] + 1) % values.shape[widest]] + place[widest + 1:]
    return values.at[tuple(place)].set(smallest).at[tuple(beside)].set(largest)


def levels(own_key, dims, split, low, largest):
    gain = 1.0
    for position, shards_of in split:
        draws = jax.random.uniform(jax.random.fold_in(jax.random.fold_in(own_key, 6), position), (shards_of,), jnp.float32, low / len(split), largest / len(split))
        gain = gain * jnp.repeat(jnp.exp(draws), dims[position] // shards_of).reshape((-1,) + (1,) * (len(dims) - 1 - position))
    return gain


def normal_values(stream_key, shape, deviation, bound, pieces=(), kind=jnp.bfloat16):
    level = levels(stream_key, shape, pieces, -0.22, 0.18) if pieces else 1.0
    array = jax.random.normal(stream_key, shape, jnp.float32) * deviation * level
    return jnp.minimum(jnp.maximum(array, -bound), bound).astype(kind)


def setup_inputs(seed: int = 0, part: int = 0) -> dict:
    seeds = jax.random.split(jax.random.key(seed), 10)
    own_keys = jax.random.split(jax.random.fold_in(seeds[9], part), 10)
    return {
        "p_blocks": normal_values(own_keys[0], (NBLOCKS, N_BLK, KP, BS, BS), (N_BLK * KP * BS) ** -0.5, 0.1875, ((0, 8),)),
        "p_cols": place_ends(jax.random.randint(own_keys[1], (NBLOCKS, N_BLK, KP), 0, REG_BLOCKS), jax.random.fold_in(own_keys[1], 1), 0, REG_BLOCKS - 1).astype(jnp.int32),
        "l_blocks": normal_values(own_keys[2], (NBLOCKS, N_BLK, KL, BS, BS), (N_BLK * KL * BS) ** -0.5, 0.1875, ((0, 8),)),
        "l_cols": place_ends(jax.random.randint(own_keys[3], (NBLOCKS, N_BLK, KL), 0, REG_BLOCKS), jax.random.fold_in(own_keys[3], 1), 0, REG_BLOCKS - 1).astype(jnp.int32),
        "charges": normal_values(own_keys[4], (FREQS, 2, PANELS), 1.0, 6.0, ((0, 2), (2, 8))),
        "currents": normal_values(own_keys[5], (FREQS, 2, CELLS), 1.0, 6.0, ((0, 2), (2, 8))),
        "omegas": jnp.clip(jnp.exp(math.log(4.0) - 2.0794415 * jax.random.uniform(seeds[6], (FREQS,), jnp.float32) ** levels(seeds[6], (FREQS,), ((0, 2),), -0.2, 0.2)), 0.5, 4.0),
        "resist": jnp.clip(jnp.exp(math.log(2.0) - 3.6888794 * jax.random.uniform(own_keys[7], (CELLS,), jnp.float32) ** levels(own_keys[7], (CELLS,), ((0, 8),), -0.2, 0.2)), 0.05, 2.0),
        "branch_ends": place_ends(jax.random.randint(own_keys[8], (2, CELLS), 0, REGION), jax.random.fold_in(own_keys[8], 1), 0, REGION - 1).astype(jnp.int32),
    }


def block_product(slabs, columns, vectors, reg_blocks):
    shifts = jnp.arange(N_BLK, dtype=jnp.int32)[:, None] * reg_blocks

    def one_row(pair):
        slab, index_set = pair
        picked_cols = (index_set.astype(jnp.int32) + shifts).astype(jnp.int32)
        picked = vectors[:, picked_cols].astype(jnp.float32)
        return jnp.einsum('skab,fskb->fa', slab.astype(jnp.float32), picked)

    result = lax.map(one_row, (slabs, columns))
    return jnp.transpose(result, (1, 0, 2)).reshape(result.shape[1], -1)


def reference(p_blocks, p_cols, l_blocks, l_cols, charges, currents, omegas, resist, branch_ends):
    col_rows = 2 * FREQS
    charge_mat = charges.reshape(col_rows, -1, BS)
    current_mat = currents.reshape(col_rows, -1, BS)
    potential = block_product(p_blocks, p_cols, charge_mat, REG_BLOCKS).astype(jnp.bfloat16)
    flux = block_product(l_blocks, l_cols, current_mat, REG_BLOCKS).reshape(FREQS, 2, -1)
    base = (jnp.arange(CELLS, dtype=jnp.int32) // REGION) * REGION
    source = (branch_ends[0] + base).astype(jnp.int32)
    target = (branch_ends[1] + base).astype(jnp.int32)
    drop = potential[:, source].astype(jnp.float32) - potential[:, target].astype(jnp.float32)
    drop = drop.reshape(FREQS, 2, -1)
    current_f = currents.astype(jnp.float32)
    scale = omegas[:, None]
    cell_re = resist * current_f[:, 0] - scale * flux[:, 1] + drop[:, 0]
    cell_im = resist * current_f[:, 1] + scale * flux[:, 0] + drop[:, 1]
    cell_rows = jnp.stack([cell_re, cell_im], axis=1)
    flat_cur = current_f.reshape(col_rows, -1).T
    outflow = jax.ops.segment_sum(flat_cur, source, PANELS) - jax.ops.segment_sum(flat_cur, target, PANELS)
    outflow = outflow.T.reshape(FREQS, 2, -1)
    charge_f = charges.astype(jnp.float32)
    panel_re = outflow[:, 0] - scale * charge_f[:, 1]
    panel_im = outflow[:, 1] + scale * charge_f[:, 0]
    panel_rows = jnp.stack([panel_re, panel_im], axis=1)
    return (cell_rows, panel_rows)
```

```python
import functools

import jax
import jax.numpy as jnp
from jax import lax
from jax.experimental import pallas as pl
from jax.experimental.pallas import tpu as pltpu
from jax.sharding import PartitionSpec as P

MESH = pl.DeviceIdType.MESH
NT = (((1,), (1,)), ((), ()))
NN = (((1,), (0,)), ((), ()))


def dot(a, b, dims):
    return lax.dot_general(a, b, dims, preferred_element_type=jnp.float32)


def quarter_turn(x):
    rows = x.shape[0]
    even = lax.broadcasted_iota(jnp.int32, x.shape, 0) % 2 == 0
    return jnp.where(even, -pltpu.roll(x, rows - 1, 0), pltpu.roll(x, 1, 0))


def kernel(n_blk, n_cell, p_cols, l_cols, omegas, resist, ends, charges, currents, p_hbm, l_hbm,
           cell_out, panel_out, *scratch):
    a_bufs, b_bufs = scratch[:n_blk], scratch[n_blk : 2 * n_blk]
    (p_buf, l_buf, inc, phi, part_out, part_in, load_sem, a_send, a_recv, b_send, b_recv,
     phi_send, phi_recv, part_send, part_recv) = scratch[2 * n_blk :]
    rows, share = charges.shape
    local = share // 128
    my_blk, my_cell = lax.axis_index("blk"), lax.axis_index("cell")

    p_load = pltpu.make_async_copy(p_hbm, p_buf, load_sem.at[0])
    l_load = pltpu.make_async_copy(l_hbm, l_buf, load_sem.at[1])
    p_load.start()
    l_load.start()

    barrier = pltpu.get_barrier_semaphore()
    for d in range(1, n_blk):
        pl.semaphore_signal(barrier, device_id={"blk": lax.rem(my_blk + d, n_blk)}, device_id_type=MESH)
    for c in range(1, n_cell):
        pl.semaphore_signal(barrier, device_id={"cell": lax.rem(my_cell + c, n_cell)}, device_id_type=MESH)

    q32 = charges[...].astype(jnp.float32)
    i32 = currents[...].astype(jnp.float32)
    i16 = currents[...]
    mixed = jnp.concatenate([q32, i32[16:]], axis=0).astype(jnp.bfloat16)
    mine = pl.ds(my_cell * local, local)
    for b in range(local):
        cols = slice(b * 128, (b + 1) * 128)
        a_bufs[0][my_cell * local + b] = mixed[:, cols]
        b_bufs[0][my_cell * local + b] = i16[:16, cols]

    pl.semaphore_wait(barrier, n_blk - 1 + n_cell - 1)

    def along_blk(bufs, send, recv, d):
        return pltpu.make_async_remote_copy(
            src_ref=bufs[0].at[mine], dst_ref=bufs[d].at[mine],
            send_sem=send.at[d, 0], recv_sem=recv.at[d, 0],
            device_id={"blk": lax.rem(my_blk + d, n_blk)}, device_id_type=MESH)

    def along_cell(bufs, send, recv, d, c):
        return pltpu.make_async_remote_copy(
            src_ref=bufs[d].at[mine], dst_ref=bufs[d].at[mine],
            send_sem=send.at[d, c], recv_sem=recv.at[d, c],
            device_id={"cell": lax.rem(my_cell + c, n_cell)}, device_id_type=MESH)

    order = sorted(range(1, n_blk), key=lambda d: min(d, n_blk - d))
    hops = range(1, n_cell)
    a_set, b_set = (a_bufs, a_send, a_recv), (b_bufs, b_send, b_recv)
    for group in (a_set, b_set):
        for d in order[::-1]:
            along_blk(*group, d).start()
        for c in hops:
            along_cell(*group, 0, c).start()

    start = ends[0:1, :]
    stop = ends[1:2, :]
    chunk = 128
    base = lax.broadcasted_iota(jnp.int32, (chunk, share), 0)

    def fill(t, carry):
        offset = pl.multiple_of(t * chunk, chunk)
        plus = jnp.where(base == start - offset, 1.0, 0.0)
        minus = jnp.where(base == stop - offset, 1.0, 0.0)
        inc[pl.ds(offset, chunk), :] = (plus - minus).astype(jnp.bfloat16)
        return carry

    lax.fori_loop(0, n_cell * share // chunk, fill, 0)

    def inc_of(owner):
        return inc[pl.ds(pl.multiple_of(owner * share, share), share), :]

    def part_copy(c):
        return pltpu.make_async_remote_copy(
            src_ref=part_out.at[c], dst_ref=part_in.at[c],
            send_sem=part_send.at[c], recv_sem=part_recv.at[c],
            device_id={"cell": lax.rem(my_cell + c, n_cell)}, device_id_type=MESH)

    for c in hops:
        owner = lax.rem(my_cell + c, n_cell)
        part_out[c] = dot(i16, inc_of(owner), NT).astype(jnp.bfloat16)
        part_copy(c).start()

    for d in order:
        along_blk(*a_set, d).wait_recv()
        for c in hops:
            along_cell(*a_set, d, c).start()

    outflow = dot(i16, inc_of(my_cell), NT)
    row = lax.broadcasted_iota(jnp.int32, (rows, 128), 0) // 2
    omega = jnp.zeros((rows, 128), jnp.float32)
    for f in range(rows // 2):
        omega = jnp.where(row == f, omegas[f], omega)
    omega = jnp.concatenate([omega] * local, axis=1)

    def add_products(acc, blocks, cols, d, pick):
        source = lax.rem(my_blk + n_blk - d, n_blk)
        for r in range(local):
            left = jnp.concatenate([pick(d, cols[r, source, k]) for k in range(2)], axis=1)
            right = jnp.concatenate([blocks[r, source, k] for k in range(2)], axis=1)
            term = dot(left, right, NT)
            acc[r] = term if acc[r] is None else acc[r] + term

    def pick_q(d, j):
        return a_bufs[d][j]

    def pick_i(d, j):
        return jnp.concatenate([b_bufs[d][j], a_bufs[d][j, 16:]], axis=0)

    for c in hops:
        along_cell(*a_set, 0, c).wait_recv()
    p_load.wait()
    acc = [None] * local
    add_products(acc, p_buf, p_cols, 0, pick_q)

    for d in order:
        along_blk(*b_set, d).wait_recv()
        for c in hops:
            along_cell(*b_set, d, c).start()
    for d in order:
        for c in hops:
            along_cell(*a_set, d, c).wait_recv()
        add_products(acc, p_buf, p_cols, d, pick_q)

    phi[0] = jnp.concatenate(acc, axis=1).astype(jnp.bfloat16)

    def phi_copy(c):
        return pltpu.make_async_remote_copy(
            src_ref=phi.at[0], dst_ref=phi.at[c],
            send_sem=phi_send.at[c], recv_sem=phi_recv.at[c],
            device_id={"cell": lax.rem(my_cell + c, n_cell)}, device_id_type=MESH)

    for c in hops:
        phi_copy(c).start()

    for c in hops:
        along_cell(*b_set, 0, c).wait_recv()
    l_load.wait()
    acc = [None] * local
    add_products(acc, l_buf, l_cols, 0, pick_i)
    for d in order:
        for c in hops:
            along_cell(*b_set, d, c).wait_recv()
        add_products(acc, l_buf, l_cols, d, pick_i)
    flux = jnp.concatenate(acc, axis=1)
    flux = jnp.concatenate([flux[:16], flux[24:]], axis=0)
    cell = resist[...] * i32 + omega * quarter_turn(flux)
    drop = dot(phi[0], inc_of(my_cell), NN)

    for c in hops:
        part_copy(c).wait_recv()
        outflow += part_in[c].astype(jnp.float32)
    panel_out[...] = outflow + omega * quarter_turn(q32)

    for c in hops:
        phi_copy(c).wait_recv()
        drop += dot(phi[c], inc_of(lax.rem(my_cell + n_cell - c, n_cell)), NN)
    cell_out[...] = cell + drop[:rows]

    for c in hops:
        part_copy(c).wait_send()
        phi_copy(c).wait_send()
    for group in (a_set, b_set):
        for d in order:
            along_blk(*group, d).wait_send()
        for d in range(n_blk):
            for c in hops:
                along_cell(*group, d, c).wait_send()


def per_device(p_blocks, p_cols, l_blocks, l_cols, charges, currents, omegas, resist, branch_ends):
    n_blk, n_cell = lax.axis_size("blk"), lax.axis_size("cell")
    freq_count, _, share = charges.shape
    rows = 2 * freq_count
    reg_blocks = n_cell * share // 128
    vmem = pl.BlockSpec(memory_space=pltpu.VMEM)
    smem = pl.BlockSpec(memory_space=pltpu.SMEM)
    hbm = pl.BlockSpec(memory_space=pltpu.HBM)
    dma = pltpu.SemaphoreType.DMA
    outs = pl.pallas_call(
        functools.partial(kernel, n_blk, n_cell),
        out_shape=[jax.ShapeDtypeStruct((rows, share), jnp.float32)] * 2,
        in_specs=[smem, smem, smem, vmem, vmem, vmem, vmem, hbm, hbm],
        out_specs=[vmem, vmem],
        scratch_shapes=[pltpu.VMEM((reg_blocks, 32, 128), jnp.bfloat16)] * n_blk
        + [pltpu.VMEM((reg_blocks, 16, 128), jnp.bfloat16)] * n_blk
        + [
            pltpu.VMEM(p_blocks.shape, p_blocks.dtype),
            pltpu.VMEM(l_blocks.shape, l_blocks.dtype),
            pltpu.VMEM((n_cell * share, share), jnp.bfloat16),
            pltpu.VMEM((n_cell, 32, share), jnp.bfloat16),
            pltpu.VMEM((n_cell, rows, share), jnp.bfloat16),
            pltpu.VMEM((n_cell, rows, share), jnp.bfloat16),
            dma((2,)),
            dma((n_blk, n_cell)), dma((n_blk, n_cell)),
            dma((n_blk, n_cell)), dma((n_blk, n_cell)),
            dma((n_cell,)), dma((n_cell,)),
            dma((n_cell,)), dma((n_cell,)),
        ],
        compiler_params=pltpu.CompilerParams(
            collective_id=0, has_side_effects=True, vmem_limit_bytes=40 * 2**20
        ),
    )(
        p_cols, l_cols, omegas, resist.reshape(1, share), branch_ends,
        charges.reshape(rows, share), currents.reshape(rows, share), p_blocks, l_blocks,
    )
    return tuple(o.reshape(freq_count, 2, share) for o in outs)


def solution(mesh):
    across = ("job", "blk", "cell")
    placed = (
        P(across, None, None, None, None),
        P(across, None, None),
        P(across, None, None, None, None),
        P(across, None, None),
        P("col", None, across),
        P("col", None, across),
        P("col"),
        P(across),
        P(None, across),
    )
    return jax.shard_map(
        per_device,
        mesh=mesh,
        in_specs=placed,
        out_specs=(P("col", None, across), P("col", None, across)),
        check_vma=False,
    )
```

```python
import functools

import jax
import jax.numpy as jnp
from jax import lax
from jax.experimental import pallas as pl
from jax.experimental.pallas import tpu as pltpu
from jax.sharding import PartitionSpec as P

MESH = pl.DeviceIdType.MESH
NT = (((1,), (1,)), ((), ()))
NN = (((1,), (0,)), ((), ()))


def dot(a, b, dims):
    return lax.dot_general(a, b, dims, preferred_element_type=jnp.float32)


def quarter_turn(x):
    rows = x.shape[0]
    even = lax.broadcasted_iota(jnp.int32, x.shape, 0) % 2 == 0
    return jnp.where(even, -pltpu.roll(x, rows - 1, 0), pltpu.roll(x, 1, 0))


def kernel(n_blk, n_cell, *refs):
    sources, both, scratch = refs[:9], refs[9], refs[10:]
    cell_out, panel_out = both.at[0], both.at[1]
    a_bufs, b_bufs = scratch[:n_blk], scratch[n_blk : 2 * n_blk]
    targets = scratch[2 * n_blk : 2 * n_blk + 9]
    charges, currents, ends, resist, omegas, p_cols, l_cols, p_buf, l_buf = targets
    (inc, phi, part_out, part_in, load_sem, a_send, a_recv, b_send, b_recv,
     phi_send, phi_recv, part_send, part_recv) = scratch[2 * n_blk + 9 :]
    rows, share = 2 * charges.shape[0], charges.shape[2]
    local = share // 128
    my_blk, my_cell = lax.axis_index("blk"), lax.axis_index("cell")

    barrier = pltpu.get_barrier_semaphore()
    peers = [(d, c) for d in range(n_blk) for c in range(n_cell) if (d or c) and not (d and c)]

    def device(d, c):
        return {"blk": lax.rem(my_blk + d, n_blk), "cell": lax.rem(my_cell + c, n_cell)}

    for d, c in peers:
        pl.semaphore_signal(barrier, device_id=device(d, c), device_id_type=MESH)

    loads = [
        pltpu.make_async_copy(src, dst, load_sem.at[i])
        for i, (src, dst) in enumerate(zip(sources, targets))
    ]
    for load in loads[:2]:
        load.start()

    for load in loads[:2]:
        load.wait()
    q32 = charges[...].astype(jnp.float32).reshape(rows, share)
    i32 = currents[...].astype(jnp.float32).reshape(rows, share)
    q16 = q32.astype(jnp.bfloat16)
    i16 = i32.astype(jnp.bfloat16)
    mine = pl.ds(my_cell * local, local)
    for b in range(local):
        cols = slice(b * 128, (b + 1) * 128)
        a_bufs[0][my_cell * local + b] = q16[:, cols]
        b_bufs[0][my_cell * local + b] = i16[:, cols]

    pl.semaphore_wait(barrier, len(peers))

    def send(group, d, c, straight):
        bufs, sent, landed = group
        source, to = (bufs[0], device(d, c)) if straight else (bufs[d], device(0, c))
        return pltpu.make_async_remote_copy(
            src_ref=source.at[mine], dst_ref=bufs[d].at[mine],
            send_sem=sent.at[d, c], recv_sem=landed.at[d, c],
            device_id=to, device_id_type=MESH)

    def along_blk(group, d):
        return send(group, d, 0, True)

    def along_cell(group, d, c):
        return send(group, d, c, False)

    order = sorted(range(1, n_blk), key=lambda d: min(d, n_blk - d))
    hops = range(1, n_cell)
    a_set, b_set = (a_bufs, a_send, a_recv), (b_bufs, b_send, b_recv)
    for group in (a_set, b_set):
        for d in order[::-1]:
            along_blk(group, d).start()
        for c in hops:
            along_cell(group, 0, c).start()
    for load in loads[2:]:
        load.start()

    for load in loads[2:7]:
        load.wait()
    start = ends[0:1, :]
    stop = ends[1:2, :]
    chunk = 128
    base = lax.broadcasted_iota(jnp.int32, (chunk, share), 0)

    def fill(t, carry):
        offset = pl.multiple_of(t * chunk, chunk)
        plus = jnp.where(base == start - offset, 1.0, 0.0)
        minus = jnp.where(base == stop - offset, 1.0, 0.0)
        inc[pl.ds(offset, chunk), :] = (plus - minus).astype(jnp.bfloat16)
        return carry

    lax.fori_loop(0, n_cell * share // chunk, fill, 0)

    def inc_of(owner):
        return inc[pl.ds(pl.multiple_of(owner * share, share), share), :]

    def part_copy(c):
        return pltpu.make_async_remote_copy(
            src_ref=part_out.at[c], dst_ref=part_in.at[c],
            send_sem=part_send.at[c], recv_sem=part_recv.at[c],
            device_id={"cell": lax.rem(my_cell + c, n_cell)}, device_id_type=MESH)

    for c in hops:
        owner = lax.rem(my_cell + c, n_cell)
        part_out[c] = dot(i16, inc_of(owner), NT).astype(jnp.bfloat16)

    def pass_on(group):
        for d in order:
            along_blk(group, d).wait_recv()
            for c in hops:
                along_cell(group, d, c).start()

    pass_on(a_set)

    outflow = dot(i16, inc_of(my_cell), NT)
    row = lax.broadcasted_iota(jnp.int32, (rows, 128), 0) // 2
    omega = jnp.zeros((rows, 128), jnp.float32)
    for f in range(rows // 2):
        omega = jnp.where(row == f, omegas[f], omega)
    omega = jnp.concatenate([omega] * local, axis=1)

    def add_products(acc, blocks, cols, d, pick):
        source = lax.rem(my_blk + n_blk - d, n_blk)
        for r in range(local):
            left = jnp.concatenate([pick(d, cols[r, k, source]) for k in range(2)], axis=1)
            right = jnp.concatenate([blocks[r, source, k] for k in range(2)], axis=1)
            term = dot(left, right, NT)
            acc[r] = term if acc[r] is None else acc[r] + term

    def pick_q(d, j):
        return a_bufs[d][j]

    def pick_i(d, j):
        return b_bufs[d][j]

    for c in hops:
        along_cell(a_set, 0, c).wait_recv()
    loads[7].wait()
    acc = [None] * local
    add_products(acc, p_buf, p_cols, 0, pick_q)

    pass_on(b_set)
    for d in order:
        for c in hops:
            along_cell(a_set, d, c).wait_recv()
        add_products(acc, p_buf, p_cols, d, pick_q)

    phi[0] = jnp.concatenate(acc, axis=1).astype(jnp.bfloat16)

    def phi_copy(c):
        return pltpu.make_async_remote_copy(
            src_ref=phi.at[0], dst_ref=phi.at[c],
            send_sem=phi_send.at[c], recv_sem=phi_recv.at[c],
            device_id={"cell": lax.rem(my_cell + c, n_cell)}, device_id_type=MESH)

    for c in hops:
        phi_copy(c).start()
    for c in hops:
        part_copy(c).start()

    for c in hops:
        along_cell(b_set, 0, c).wait_recv()
    loads[8].wait()
    acc = [None] * local
    add_products(acc, l_buf, l_cols, 0, pick_i)
    for d in order:
        for c in hops:
            along_cell(b_set, d, c).wait_recv()
        add_products(acc, l_buf, l_cols, d, pick_i)
    flux = jnp.concatenate(acc, axis=1)
    cell = resist[...] * i32 + omega * quarter_turn(flux)
    drop = dot(phi[0], inc_of(my_cell), NN)

    for c in hops:
        part_copy(c).wait_recv()
        outflow += part_in[c].astype(jnp.float32)
    panel_out[...] = (outflow + omega * quarter_turn(q32)).reshape(panel_out.shape)

    for c in hops:
        phi_copy(c).wait_recv()
        drop += dot(phi[c], inc_of(lax.rem(my_cell + n_cell - c, n_cell)), NN)
    cell_out[...] = (cell + drop).reshape(cell_out.shape)

    for c in hops:
        part_copy(c).wait_send()
        phi_copy(c).wait_send()
    for group in (a_set, b_set):
        for d in order:
            along_blk(group, d).wait_send()
        for d in range(n_blk):
            for c in hops:
                along_cell(group, d, c).wait_send()


def per_device(p_blocks, p_cols, l_blocks, l_cols, charges, currents, omegas, resist, branch_ends):
    n_blk, n_cell = lax.axis_size("blk"), lax.axis_size("cell")
    freq_count, _, share = charges.shape
    rows = 2 * freq_count
    reg_blocks = n_cell * share // 128
    vmem = pl.BlockSpec(memory_space=pltpu.VMEM)
    operands = (
        charges, currents, branch_ends, resist.reshape(1, share), omegas,
        p_cols.transpose(0, 2, 1), l_cols.transpose(0, 2, 1), p_blocks, l_blocks,
    )
    spaces = [pltpu.VMEM] * 4 + [pltpu.SMEM] * 3 + [pltpu.VMEM] * 2
    dma = pltpu.SemaphoreType.DMA
    outs = pl.pallas_call(
        functools.partial(kernel, n_blk, n_cell),
        out_shape=pltpu.VMEM((2, freq_count, 2, share), jnp.float32),
        in_specs=[pl.BlockSpec(memory_space=pltpu.HBM)] * len(operands),
        out_specs=vmem,
        scratch_shapes=[pltpu.VMEM((reg_blocks, rows, 128), jnp.bfloat16)] * n_blk
        + [pltpu.VMEM((reg_blocks, rows, 128), jnp.bfloat16)] * n_blk
        + [space(x.shape, x.dtype) for space, x in zip(spaces, operands)]
        + [
            pltpu.VMEM((n_cell * share, share), jnp.bfloat16),
            pltpu.VMEM((n_cell, rows, share), jnp.bfloat16),
            pltpu.VMEM((n_cell, rows, share), jnp.bfloat16),
            pltpu.VMEM((n_cell, rows, share), jnp.bfloat16),
            dma((len(operands),)),
            dma((n_blk, n_cell)), dma((n_blk, n_cell)),
            dma((n_blk, n_cell)), dma((n_blk, n_cell)),
            dma((n_cell,)), dma((n_cell,)),
            dma((n_cell,)), dma((n_cell,)),
        ],
        compiler_params=pltpu.CompilerParams(
            collective_id=0, has_side_effects=True, vmem_limit_bytes=60 * 2**20
        ),
    )(*[pltpu.with_memory_space_constraint(x, pltpu.HBM) for x in operands])
    return outs[0], outs[1]


def solution(mesh):
    across = ("job", "blk", "cell")
    placed = (
        P(across, None, None, None, None),
        P(across, None, None),
        P(across, None, None, None, None),
        P(across, None, None),
        P("col", None, across),
        P("col", None, across),
        P("col"),
        P(across),
        P(None, across),
    )
    return jax.shard_map(
        per_device,
        mesh=mesh,
        in_specs=placed,
        out_specs=(P("col", None, across), P("col", None, across)),
        check_vma=False,
    )
```

```python
import functools

import jax
import jax.numpy as jnp
from jax import lax
from jax.experimental import pallas as pl
from jax.experimental.pallas import tpu as pltpu
from jax.sharding import PartitionSpec as P

MESH = pl.DeviceIdType.MESH
NT = (((1,), (1,)), ((), ()))
NN = (((1,), (0,)), ((), ()))


def dot(a, b, dims):
    return lax.dot_general(a, b, dims, preferred_element_type=jnp.float32)


def quarter_turn(x):
    rows = x.shape[0]
    even = lax.broadcasted_iota(jnp.int32, x.shape, 0) % 2 == 0
    return jnp.where(even, -pltpu.roll(x, rows - 1, 0), pltpu.roll(x, 1, 0))


def kernel(n_blk, n_cell, *refs):
    sources, both, scratch = refs[:9], refs[9], refs[10:]
    cell_out, panel_out = both.at[0], both.at[1]
    a_bufs, b_bufs = scratch[:n_blk], scratch[n_blk : 2 * n_blk]
    targets = scratch[2 * n_blk : 2 * n_blk + 9]
    charges, currents, ends, resist, omegas, p_cols, l_cols, p_buf, l_buf = targets
    (acc, inc, phi, part_out, part_in, load_sem, a_send, a_recv, b_send, b_recv,
     phi_send, phi_recv, part_send, part_recv) = scratch[2 * n_blk + 9 :]
    rows, share = 2 * charges.shape[0], charges.shape[2]
    local = share // 128
    my_blk, my_cell = lax.axis_index("blk"), lax.axis_index("cell")

    barrier = pltpu.get_barrier_semaphore()
    peers = [(d, c) for d in range(n_blk) for c in range(n_cell) if (d or c) and not (d and c)]

    def device(d, c):
        return {"blk": lax.rem(my_blk + d, n_blk), "cell": lax.rem(my_cell + c, n_cell)}

    for d, c in peers:
        pl.semaphore_signal(barrier, device_id=device(d, c), device_id_type=MESH)

    loads = [
        pltpu.make_async_copy(src, dst, load_sem.at[i])
        for i, (src, dst) in enumerate(zip(sources, targets))
    ]
    for load in loads[:2]:
        load.start()

    for load in loads[:2]:
        load.wait()
    q32 = charges[...].astype(jnp.float32).reshape(rows, share)
    i32 = currents[...].astype(jnp.float32).reshape(rows, share)
    q16 = q32.astype(jnp.bfloat16)
    i16 = i32.astype(jnp.bfloat16)
    mine = pl.ds(my_cell * local, local)
    for b in range(local):
        cols = slice(b * 128, (b + 1) * 128)
        a_bufs[0][my_cell * local + b] = q16[:, cols]
        b_bufs[0][my_cell * local + b] = i16[:, cols]

    pl.semaphore_wait(barrier, len(peers))

    def send(group, d, c, straight):
        bufs, sent, landed = group
        source, to = (bufs[0], device(d, c)) if straight else (bufs[d], device(0, c))
        return pltpu.make_async_remote_copy(
            src_ref=source.at[mine], dst_ref=bufs[d].at[mine],
            send_sem=sent.at[d, c], recv_sem=landed.at[d, c],
            device_id=to, device_id_type=MESH)

    def along_blk(group, d):
        return send(group, d, 0, True)

    def along_cell(group, d, c):
        return send(group, d, c, False)

    order = sorted(range(1, n_blk), key=lambda d: min(d, n_blk - d))

    def by_distance(distances, step, sending):
        for dist in distances:
            back, on = (n_blk - dist, dist) if sending else (dist, n_blk - dist)
            pl.when(my_blk >= dist)(functools.partial(step, back))
            pl.when(my_blk + dist < n_blk)(functools.partial(step, on))

    hops = range(1, n_cell)
    a_set, b_set = (a_bufs, a_send, a_recv), (b_bufs, b_send, b_recv)
    for group in (a_set, b_set):
        for c in hops:
            along_cell(group, 0, c).start()
        by_distance(range(n_blk - 1, 0, -1), lambda d: along_blk(group, d).start(), True)
    for load in loads[2:]:
        load.start()

    for load in loads[2:7]:
        load.wait()
    start = ends[0:1, :]
    stop = ends[1:2, :]
    chunk = 128
    base = lax.broadcasted_iota(jnp.int32, (chunk, share), 0)

    def fill(t, carry):
        offset = pl.multiple_of(t * chunk, chunk)
        plus = jnp.where(base == start - offset, 1.0, 0.0)
        minus = jnp.where(base == stop - offset, 1.0, 0.0)
        inc[pl.ds(offset, chunk), :] = (plus - minus).astype(jnp.bfloat16)
        return carry

    lax.fori_loop(0, n_cell * share // chunk, fill, 0)

    def inc_of(owner):
        return inc[pl.ds(pl.multiple_of(owner * share, share), share), :]

    def part_copy(c):
        return pltpu.make_async_remote_copy(
            src_ref=part_out.at[c], dst_ref=part_in.at[c],
            send_sem=part_send.at[c], recv_sem=part_recv.at[c],
            device_id={"cell": lax.rem(my_cell + c, n_cell)}, device_id_type=MESH)

    for c in hops:
        owner = lax.rem(my_cell + c, n_cell)
        part_out[c] = dot(i16, inc_of(owner), NT).astype(jnp.bfloat16)
        part_copy(c).start()

    def pass_on(group):
        def step(d):
            along_blk(group, d).wait_recv()
            for c in hops:
                along_cell(group, d, c).start()

        by_distance(range(1, n_blk), step, False)

    pass_on(a_set)

    outflow = dot(i16, inc_of(my_cell), NT)
    row = lax.broadcasted_iota(jnp.int32, (rows, 128), 0) // 2
    omega = jnp.zeros((rows, 128), jnp.float32)
    for f in range(rows // 2):
        omega = jnp.where(row == f, omegas[f], omega)
    omega = jnp.concatenate([omega] * local, axis=1)

    def add_products(acc, blocks, cols, pick, first, d):
        source = lax.rem(my_blk + n_blk - d, n_blk)
        for r in range(local):
            left = jnp.concatenate([pick(d, cols[r, k, source]) for k in range(2)], axis=1)
            right = jnp.concatenate([blocks[r, source, k] for k in range(2)], axis=1)
            term = dot(left, right, NT)
            if first:
                acc[r] = term
            else:
                acc[r] += term

    def pick_q(d, j):
        return a_bufs[d][j]

    def pick_i(d, j):
        return b_bufs[d][j]

    for c in hops:
        along_cell(a_set, 0, c).wait_recv()
    loads[7].wait()
    add_products(acc, p_buf, p_cols, pick_q, True, 0)

    pass_on(b_set)

    def arrive_a(d):
        for c in hops:
            along_cell(a_set, d, c).wait_recv()
        add_products(acc, p_buf, p_cols, pick_q, False, d)

    by_distance(range(1, n_blk), arrive_a, False)

    phi[0] = jnp.concatenate([acc[r] for r in range(local)], axis=1).astype(jnp.bfloat16)

    def phi_copy(c):
        return pltpu.make_async_remote_copy(
            src_ref=phi.at[0], dst_ref=phi.at[c],
            send_sem=phi_send.at[c], recv_sem=phi_recv.at[c],
            device_id={"cell": lax.rem(my_cell + c, n_cell)}, device_id_type=MESH)

    for c in hops:
        phi_copy(c).start()

    for c in hops:
        along_cell(b_set, 0, c).wait_recv()
    loads[8].wait()
    add_products(acc, l_buf, l_cols, pick_i, True, 0)

    def arrive_b(d):
        for c in hops:
            along_cell(b_set, d, c).wait_recv()
        add_products(acc, l_buf, l_cols, pick_i, False, d)

    by_distance(range(1, n_blk), arrive_b, False)
    flux = jnp.concatenate([acc[r] for r in range(local)], axis=1)
    cell = resist[...] * i32 + omega * quarter_turn(flux)
    drop = dot(phi[0], inc_of(my_cell), NN)

    for c in hops:
        part_copy(c).wait_recv()
        outflow += part_in[c].astype(jnp.float32)
    panel_out[...] = (outflow + omega * quarter_turn(q32)).reshape(panel_out.shape)

    for c in hops:
        phi_copy(c).wait_recv()
        drop += dot(phi[c], inc_of(lax.rem(my_cell + n_cell - c, n_cell)), NN)
    cell_out[...] = (cell + drop).reshape(cell_out.shape)

    for c in hops:
        part_copy(c).wait_send()
        phi_copy(c).wait_send()
    for group in (a_set, b_set):
        for d in order:
            along_blk(group, d).wait_send()
        for d in range(n_blk):
            for c in hops:
                along_cell(group, d, c).wait_send()


def per_device(p_blocks, p_cols, l_blocks, l_cols, charges, currents, omegas, resist, branch_ends):
    n_blk, n_cell = lax.axis_size("blk"), lax.axis_size("cell")
    freq_count, _, share = charges.shape
    rows = 2 * freq_count
    reg_blocks = n_cell * share // 128
    vmem = pl.BlockSpec(memory_space=pltpu.VMEM)
    operands = (
        charges, currents, branch_ends, resist.reshape(1, share), omegas,
        p_cols.transpose(0, 2, 1), l_cols.transpose(0, 2, 1), p_blocks, l_blocks,
    )
    spaces = [pltpu.VMEM] * 4 + [pltpu.SMEM] * 3 + [pltpu.VMEM] * 2
    dma = pltpu.SemaphoreType.DMA
    outs = pl.pallas_call(
        functools.partial(kernel, n_blk, n_cell),
        out_shape=pltpu.VMEM((2, freq_count, 2, share), jnp.float32),
        in_specs=[pl.BlockSpec(memory_space=pltpu.HBM)] * len(operands),
        out_specs=vmem,
        scratch_shapes=[pltpu.VMEM((reg_blocks, rows, 128), jnp.bfloat16)] * n_blk
        + [pltpu.VMEM((reg_blocks, rows, 128), jnp.bfloat16)] * n_blk
        + [space(x.shape, x.dtype) for space, x in zip(spaces, operands)]
        + [
            pltpu.VMEM((share // 128, rows, 128), jnp.float32),
            pltpu.VMEM((n_cell * share, share), jnp.bfloat16),
            pltpu.VMEM((n_cell, rows, share), jnp.bfloat16),
            pltpu.VMEM((n_cell, rows, share), jnp.bfloat16),
            pltpu.VMEM((n_cell, rows, share), jnp.bfloat16),
            dma((len(operands),)),
            dma((n_blk, n_cell)), dma((n_blk, n_cell)),
            dma((n_blk, n_cell)), dma((n_blk, n_cell)),
            dma((n_cell,)), dma((n_cell,)),
            dma((n_cell,)), dma((n_cell,)),
        ],
        compiler_params=pltpu.CompilerParams(
            collective_id=0, has_side_effects=True, vmem_limit_bytes=60 * 2**20
        ),
    )(*[pltpu.with_memory_space_constraint(x, pltpu.HBM) for x in operands])
    return outs[0], outs[1]


def solution(mesh):
    across = ("job", "blk", "cell")
    placed = (
        P(across, None, None, None, None),
        P(across, None, None),
        P(across, None, None, None, None),
        P(across, None, None),
        P("col", None, across),
        P("col", None, across),
        P("col"),
        P(across),
        P(None, across),
    )
    return jax.shard_map(
        per_device,
        mesh=mesh,
        in_specs=placed,
        out_specs=(P("col", None, across), P("col", None, across)),
        check_vma=False,
    )
```

```python
import functools

import jax
import jax.numpy as jnp
from jax import lax
from jax.experimental import pallas as pl
from jax.experimental.pallas import tpu as pltpu
from jax.sharding import PartitionSpec as P

MESH = pl.DeviceIdType.MESH
NT = (((1,), (1,)), ((), ()))
NN = (((1,), (0,)), ((), ()))


def dot(a, b, dims):
    return lax.dot_general(a, b, dims, preferred_element_type=jnp.float32)


def quarter_turn(x):
    rows = x.shape[0]
    even = lax.broadcasted_iota(jnp.int32, x.shape, 0) % 2 == 0
    return jnp.where(even, -pltpu.roll(x, rows - 1, 0), pltpu.roll(x, 1, 0))


def kernel(n_blk, n_cell, *refs):
    sources, both, scratch = refs[:9], refs[9], refs[10:]
    cell_out, panel_out = both.at[0], both.at[1]
    a_bufs, b_bufs = scratch[:n_blk], scratch[n_blk : 2 * n_blk]
    targets = scratch[2 * n_blk : 2 * n_blk + 9]
    charges, currents, ends, resist, omegas, p_cols, l_cols, p_buf, l_buf = targets
    (acc, inc, phi, part_out, part_in, load_sem, a_send, a_recv, b_send, b_recv,
     phi_send, phi_recv, part_send, part_recv) = scratch[2 * n_blk + 9 :]
    rows, share = 2 * charges.shape[0], charges.shape[2]
    local = share // 128
    my_blk, my_cell = lax.axis_index("blk"), lax.axis_index("cell")

    barrier = pltpu.get_barrier_semaphore()
    peers = [(d, c) for d in range(n_blk) for c in range(n_cell) if (d or c) and not (d and c)]

    def device(d, c):
        return {"blk": lax.rem(my_blk + d, n_blk), "cell": lax.rem(my_cell + c, n_cell)}

    for d, c in peers:
        pl.semaphore_signal(barrier, device_id=device(d, c), device_id_type=MESH)

    loads = [
        pltpu.make_async_copy(src, dst, load_sem.at[i])
        for i, (src, dst) in enumerate(zip(sources, targets))
    ]
    for load in loads[:2]:
        load.start()

    for load in loads[:2]:
        load.wait()
    q32 = charges[...].astype(jnp.float32).reshape(rows, share)
    i32 = currents[...].astype(jnp.float32).reshape(rows, share)
    q16 = q32.astype(jnp.bfloat16)
    i16 = i32.astype(jnp.bfloat16)
    mine = pl.ds(my_cell * local, local)
    for b in range(local):
        cols = slice(b * 128, (b + 1) * 128)
        a_bufs[0][my_cell * local + b] = q16[:, cols]
        b_bufs[0][my_cell * local + b] = i16[:, cols]

    pl.semaphore_wait(barrier, len(peers))

    def send(group, d, c, straight):
        bufs, sent, landed = group
        source, to = (bufs[0], device(d, c)) if straight else (bufs[d], device(0, c))
        return pltpu.make_async_remote_copy(
            src_ref=source.at[mine], dst_ref=bufs[d].at[mine],
            send_sem=sent.at[d, c], recv_sem=landed.at[d, c],
            device_id=to, device_id_type=MESH)

    def along_blk(group, d):
        return send(group, d, 0, True)

    def along_cell(group, d, c):
        return send(group, d, c, False)

    order = sorted(range(1, n_blk), key=lambda d: min(d, n_blk - d))

    def by_distance(distances, step, sending):
        for dist in distances:
            back, on = (n_blk - dist, dist) if sending else (dist, n_blk - dist)
            pl.when(my_blk >= dist)(functools.partial(step, back))
            pl.when(my_blk + dist < n_blk)(functools.partial(step, on))

    hops = range(1, n_cell)
    a_set, b_set = (a_bufs, a_send, a_recv), (b_bufs, b_send, b_recv)
    for group in (a_set, b_set):
        for c in hops:
            along_cell(group, 0, c).start()
        by_distance(range(n_blk - 1, 0, -1), lambda d: along_blk(group, d).start(), True)
    for load in loads[2:]:
        load.start()

    for load in loads[2:7]:
        load.wait()
    start = ends[0:1, :]
    stop = ends[1:2, :]
    chunk = 128
    base = lax.broadcasted_iota(jnp.int32, (chunk, share), 0)

    def fill(t, carry):
        offset = pl.multiple_of(t * chunk, chunk)
        plus = jnp.where(base == start - offset, 1.0, 0.0)
        minus = jnp.where(base == stop - offset, 1.0, 0.0)
        inc[pl.ds(offset, chunk), :] = (plus - minus).astype(jnp.bfloat16)
        return carry

    lax.fori_loop(0, n_cell * share // chunk, fill, 0)

    def inc_of(owner):
        return inc[pl.ds(pl.multiple_of(owner * share, share), share), :]

    def part_copy(c):
        return pltpu.make_async_remote_copy(
            src_ref=part_out.at[c], dst_ref=part_in.at[c],
            send_sem=part_send.at[c], recv_sem=part_recv.at[c],
            device_id={"cell": lax.rem(my_cell + c, n_cell)}, device_id_type=MESH)

    for c in hops:
        owner = lax.rem(my_cell + c, n_cell)
        part_out[c] = dot(i16, inc_of(owner), NT).astype(jnp.bfloat16)
        part_copy(c).start()

    def pass_on(group):
        def step(d):
            along_blk(group, d).wait_recv()
            for c in hops:
                along_cell(group, d, c).start()

        by_distance(range(1, n_blk), step, False)

    pass_on(a_set)

    outflow = dot(i16, inc_of(my_cell), NT)
    row = lax.broadcasted_iota(jnp.int32, (rows, 128), 0) // 2
    omega = jnp.zeros((rows, 128), jnp.float32)
    for f in range(rows // 2):
        omega = jnp.where(row == f, omegas[f], omega)
    omega = jnp.concatenate([omega] * local, axis=1)

    def add_products(acc, blocks, cols, pick, first, d):
        source = lax.rem(my_blk + n_blk - d, n_blk)
        for r in range(local):
            left = jnp.concatenate([pick(d, cols[r, k, source]) for k in range(2)], axis=1)
            right = jnp.concatenate([blocks[r, source, k] for k in range(2)], axis=1)
            term = dot(left, right, NT)
            if first:
                acc[r] = term
            else:
                acc[r] += term

    def pick_q(d, j):
        return a_bufs[d][j]

    def pick_i(d, j):
        return b_bufs[d][j]

    for c in hops:
        along_cell(a_set, 0, c).wait_recv()
    loads[7].wait()
    add_products(acc, p_buf, p_cols, pick_q, True, 0)

    pass_on(b_set)

    def arrive_a(d):
        for c in hops:
            along_cell(a_set, d, c).wait_recv()
        add_products(acc, p_buf, p_cols, pick_q, False, d)

    by_distance(range(1, n_blk), arrive_a, False)

    phi[0] = jnp.concatenate([acc[r] for r in range(local)], axis=1).astype(jnp.bfloat16)

    def phi_copy(c):
        return pltpu.make_async_remote_copy(
            src_ref=phi.at[0], dst_ref=phi.at[c],
            send_sem=phi_send.at[c], recv_sem=phi_recv.at[c],
            device_id={"cell": lax.rem(my_cell + c, n_cell)}, device_id_type=MESH)

    for c in hops:
        phi_copy(c).start()

    drop = dot(phi[0], inc_of(my_cell), NN)
    for c in hops:
        part_copy(c).wait_recv()
        outflow += part_in[c].astype(jnp.float32)
    panel_out[...] = (outflow + omega * quarter_turn(q32)).reshape(panel_out.shape)

    for c in hops:
        along_cell(b_set, 0, c).wait_recv()
    loads[8].wait()
    add_products(acc, l_buf, l_cols, pick_i, True, 0)

    def arrive_b(d):
        for c in hops:
            along_cell(b_set, d, c).wait_recv()
        add_products(acc, l_buf, l_cols, pick_i, False, d)

    by_distance(range(1, n_blk), arrive_b, False)
    flux = jnp.concatenate([acc[r] for r in range(local)], axis=1)
    cell = resist[...] * i32 + omega * quarter_turn(flux)


    for c in hops:
        phi_copy(c).wait_recv()
        drop += dot(phi[c], inc_of(lax.rem(my_cell + n_cell - c, n_cell)), NN)
    cell_out[...] = (cell + drop).reshape(cell_out.shape)

    for c in hops:
        part_copy(c).wait_send()
        phi_copy(c).wait_send()
    for group in (a_set, b_set):
        for d in order:
            along_blk(group, d).wait_send()
        for d in range(n_blk):
            for c in hops:
                along_cell(group, d, c).wait_send()


def per_device(p_blocks, p_cols, l_blocks, l_cols, charges, currents, omegas, resist, branch_ends):
    n_blk, n_cell = lax.axis_size("blk"), lax.axis_size("cell")
    freq_count, _, share = charges.shape
    rows = 2 * freq_count
    reg_blocks = n_cell * share // 128
    vmem = pl.BlockSpec(memory_space=pltpu.VMEM)
    operands = (
        charges, currents, branch_ends, resist.reshape(1, share), omegas,
        p_cols.transpose(0, 2, 1), l_cols.transpose(0, 2, 1), p_blocks, l_blocks,
    )
    spaces = [pltpu.VMEM] * 4 + [pltpu.SMEM] * 3 + [pltpu.VMEM] * 2
    dma = pltpu.SemaphoreType.DMA
    outs = pl.pallas_call(
        functools.partial(kernel, n_blk, n_cell),
        out_shape=pltpu.VMEM((2, freq_count, 2, share), jnp.float32),
        in_specs=[pl.BlockSpec(memory_space=pltpu.HBM)] * len(operands),
        out_specs=vmem,
        scratch_shapes=[pltpu.VMEM((reg_blocks, rows, 128), jnp.bfloat16)] * n_blk
        + [pltpu.VMEM((reg_blocks, rows, 128), jnp.bfloat16)] * n_blk
        + [space(x.shape, x.dtype) for space, x in zip(spaces, operands)]
        + [
            pltpu.VMEM((share // 128, rows, 128), jnp.float32),
            pltpu.VMEM((n_cell * share, share), jnp.bfloat16),
            pltpu.VMEM((n_cell, rows, share), jnp.bfloat16),
            pltpu.VMEM((n_cell, rows, share), jnp.bfloat16),
            pltpu.VMEM((n_cell, rows, share), jnp.bfloat16),
            dma((len(operands),)),
            dma((n_blk, n_cell)), dma((n_blk, n_cell)),
            dma((n_blk, n_cell)), dma((n_blk, n_cell)),
            dma((n_cell,)), dma((n_cell,)),
            dma((n_cell,)), dma((n_cell,)),
        ],
        compiler_params=pltpu.CompilerParams(
            collective_id=0, has_side_effects=True, vmem_limit_bytes=60 * 2**20
        ),
    )(*[pltpu.with_memory_space_constraint(x, pltpu.HBM) for x in operands])
    return outs[0], outs[1]


def solution(mesh):
    across = ("job", "blk", "cell")
    placed = (
        P(across, None, None, None, None),
        P(across, None, None),
        P(across, None, None, None, None),
        P(across, None, None),
        P("col", None, across),
        P("col", None, across),
        P("col"),
        P(across),
        P(None, across),
    )
    return jax.shard_map(
        per_device,
        mesh=mesh,
        in_specs=placed,
        out_specs=(P("col", None, across), P("col", None, across)),
        check_vma=False,
    )
```
